128 devices in a mesh: uv: 4 (over y), channel: 16 (over z, x_hi, core), parity: 2 (over x_lo).
Axes of the slice: x: 4 (x_hi: 2, x_lo: 2; x = x_hi * 2 + x_lo), y: 4, z: 4, core: 2. Of those that a mesh axis runs over, the one named last changes fastest.
Arguments:
- visibility: bfloat16 [2, 16, 128, 32, 128], P('parity', 'channel', 'uv'), may hold values from -6 to 6
- kernel: bfloat16 [2, 16, 128, 128, 256], P('parity', 'channel', 'uv'), may hold values from -0.5 to 0.5
- block_tile: int32 [2, 16, 128], P('parity', 'channel', 'uv'), may hold values from 0 to 255, as said below
- block_chan: int32 [2, 16, 128], P('parity', 'channel', 'uv'), may hold values from 0 to 48
- tile_owner: int32 [256], replicated, may hold values from 0 to 3, as said below
- inv_cov: bfloat16 [1024, 1024], replicated, as said below
Outputs:
- cross_power: float32 [1024, 65536], P(None, ('uv', 'channel', 'parity'))
- diff_power: float32 [1024, 65536], P(None, ('uv', 'channel', 'parity'))
The draws below stay inside these ranges and needn't reach their ends.
Inputs may be any that keep to these rules, and one draw needn't show every extreme that they name: `tile_owner`: each owner index owns exactly 64 tiles. `block_tile`: call slot(t) // 4 the cell group of tile t. Among the 32 blocks of one device (one aligned run along the last dimension), at most 1 name tiles of the same owner and the same cell group. `inv_cov`: entries are finite.
All inputs are finite; a program needn't handle non-finite values.
Results may differ from the reference program's by a relative error of at most 0.0067.
Values may be sent and summed in bfloat16 or wider, within the bound.
No kernel may reach another device: no remote copies, remote signals or barrier semaphores. Data moves between devices by JAX's collectives and lax.ppermute only.
A program may use at most 128 MiB of HBM per device.

```python
import math
import jax
import jax.numpy as jnp
from jax import lax

NCH = 1024
PIX = 256
CHB = 16
BV = 128
NB = 32
TILE_DEV = 64
CH_DEV = 64
TILES = 256
TPC = 4
CELLS = 65536
DESTS = 64
SLOTS = 1
BLOCKS = 128
N_UV = 4
N_CHANNEL = 16


def owner_table(key):
    ranking = jax.random.permutation(jax.random.fold_in(key, 7), TILES)
    return (ranking // TILE_DEV).astype(jnp.int32)


def draw_tile_owner(key, part):
    return owner_table(key)


def draw_block_tile(key, part):
    owners_all = owner_table(key)
    indices = jnp.arange(TILES, dtype=jnp.int32)
    listing = jnp.argsort(owners_all * TILES + indices).astype(jnp.int32)
    hot_dest = jax.random.randint(jax.random.fold_in(key, 13), (), 0, DESTS).astype(jnp.int32)
    dev_keys = jax.random.split(jax.random.fold_in(key, 17), 2 * N_CHANNEL * N_UV)

    def device_blocks(subkey):
        key_perm, key_order, key_pick = jax.random.split(subkey, 3)
        spares = jax.random.permutation(key_perm, (DESTS - 1) * SLOTS)[:NB - SLOTS] // SLOTS
        spares = spares.astype(jnp.int32)
        spares = spares + (spares >= hot_dest).astype(jnp.int32)
        target = jnp.concatenate([jnp.full((SLOTS,), hot_dest, jnp.int32), spares])
        target = jax.random.permutation(key_order, target)
        choose = jax.random.randint(key_pick, (NB,), 0, TPC).astype(jnp.int32)
        owner_pick = target // N_CHANNEL
        slot_pick = target % N_CHANNEL * TPC + choose
        return listing[owner_pick * TILE_DEV + slot_pick]
    tile_ids = jax.vmap(device_blocks)(dev_keys)
    return tile_ids.reshape(2, N_CHANNEL, N_UV * NB).astype(jnp.int32)


def draw_inv_cov(key, part):
    key_off, key_diag = jax.random.split(jax.random.fold_in(key, 31), 2)
    spread = 0.7 / math.sqrt(NCH)
    offdiag = jax.random.normal(key_off, (NCH, NCH), jnp.float32) * spread
    diagonal = jnp.exp(jax.random.uniform(key_diag, (NCH,), jnp.float32, math.log(0.5), math.log(2.0)))
    matrix = offdiag + jnp.eye(NCH, dtype=jnp.float32) * diagonal[None, :]
    return matrix.astype(jnp.bfloat16)


def set_ends(drawn, own_key, least, high):
    longest = drawn.shape.index(max(drawn.shape))
    spots = []
    for shift in (0, 1):
        where = [jax.random.randint(jax.random.fold_in(own_key, axis), (), 0, length) for axis, length in enumerate(drawn.shape)]
        where[longest] = (where[longest] + shift) % drawn.shape[longest]
        spots.append(tuple(where))
    return drawn.at[spots[0]].set(least).at[spots[1]].set(high)


def levels(stream_key, extent, shards, low, largest):
    gain = 1.0
    for dim, blocks in shards:
        draws = jax.random.uniform(jax.random.fold_in(jax.random.fold_in(stream_key, 6), dim), (blocks,), jnp.float32, low / len(shards), largest / len(shards))
        gain = gain * jnp.repeat(jnp.exp(draws), extent[dim] // blocks).reshape((-1,) + (1,) * (len(extent) - 1 - dim))
    return gain


def centred(rng, extent, scale, reach, shards=(), kind=jnp.bfloat16):
    loudness = levels(rng, extent, shards, -0.22, 0.18) if shards else 1.0
    result = jax.random.normal(rng, extent, jnp.float32) * scale * loudness
    return jnp.minimum(jnp.maximum(result, -reach), reach).astype(kind)


def setup_inputs(seed: int = 0) -> dict:
    arg_keys = jax.random.split(jax.random.key(seed), 7)
    visibility = centred(arg_keys[0], (2, N_CHANNEL, BLOCKS, 2 * CHB, BV), 1.0, 6.0, ((0, 2), (1, 16), (2, 4)))
    kernel = centred(arg_keys[1], (2, N_CHANNEL, BLOCKS, BV, PIX), BV ** -0.5, 0.5, ((0, 2), (1, 16), (2, 4)))
    block_tile = draw_block_tile(jax.random.fold_in(arg_keys[6], 71), 0)
    block_chan = set_ends(jax.random.randint(arg_keys[3], (2, N_CHANNEL, BLOCKS), 0, CH_DEV - CHB + 1), jax.random.fold_in(arg_keys[3], 1), 0, CH_DEV - CHB).astype(jnp.int32)
    tile_owner = draw_tile_owner(jax.random.fold_in(arg_keys[6], 71), 0)
    inv_cov = draw_inv_cov(jax.random.fold_in(arg_keys[6], 71), 0)
    return dict(visibility=visibility, kernel=kernel, block_tile=block_tile, block_chan=block_chan, tile_owner=tile_owner, inv_cov=inv_cov)


def delay_table(count):
    indices = jnp.arange(count, dtype=jnp.int32)
    phase_int = (indices[:, None] * indices[None, :]) % count
    angles = phase_int.astype(jnp.float32) * (2.0 * math.pi / count)
    return jnp.concatenate([jnp.cos(angles), jnp.sin(angles)], axis=0).astype(jnp.bfloat16)


def block_terms(operand_pair):
    samples, weights = operand_pair
    return jnp.einsum("bkv,bvp->bkp", samples.astype(jnp.float32), weights.astype(jnp.float32)).astype(jnp.bfloat16)


def reference(visibility, kernel, block_tile, block_chan, tile_owner, inv_cov):
    indices = jnp.arange(TILES, dtype=jnp.int32)
    same_owner = (tile_owner[:, None] == tile_owner[None, :]) & (indices[:, None] < indices[None, :])
    tile_slot = jnp.sum(same_owner.astype(jnp.int32), axis=0).astype(jnp.int32)
    tile_cell = (tile_owner * TILE_DEV + tile_slot) * PIX
    chan_offsets = jnp.arange(CHB, dtype=jnp.int32)
    pix_offsets = jnp.arange(PIX, dtype=jnp.int32)
    group_base = jnp.arange(N_CHANNEL, dtype=jnp.int32)[:, None] * CH_DEV
    all_grids = []
    for parity in range(2):
        partials = lax.map(block_terms, (visibility[parity], kernel[parity]))
        row_index = (group_base + block_chan[parity])[..., None] + chan_offsets
        col_index = tile_cell[block_tile[parity]][..., None] + pix_offsets
        values = jnp.moveaxis(partials.reshape(N_CHANNEL, BLOCKS, 2, CHB, PIX), 2, 0).astype(jnp.float32)
        gridded = jnp.zeros((2, NCH, CELLS), jnp.float32).at[:, row_index[..., None], col_index[..., None, :]].add(values)
        all_grids.append(gridded.astype(jnp.bfloat16))
    all_grids = jnp.stack(all_grids)
    dft_table = delay_table(NCH).astype(jnp.float32)
    cov_wide = inv_cov.astype(jnp.float32)
    block_cells = math.gcd(CELLS, 2048)
    block_count = CELLS // block_cells

    def spectra(block_index):
        piece = lax.dynamic_slice_in_dim(all_grids, block_index * block_cells, block_cells, 3).astype(jnp.float32)
        weighted = jnp.einsum("ij,prjc->pric", cov_wide, piece).astype(jnp.bfloat16)
        weighted = lax.optimization_barrier(weighted).astype(jnp.float32)
        projected = jnp.einsum("ij,prjc->pric", dft_table, weighted)
        spec_real = projected[:, 0, :NCH] + projected[:, 1, NCH:]
        spec_imag = projected[:, 1, :NCH] - projected[:, 0, NCH:]
        cross_power = (spec_real[0] * spec_real[1] + spec_imag[0] * spec_imag[1]) / NCH
        real_gap = spec_real[0] - spec_real[1]
        imag_gap = spec_imag[0] - spec_imag[1]
        diff_power = (real_gap * real_gap + imag_gap * imag_gap) / NCH
        return cross_power, diff_power

    cross_blocks, diff_blocks = lax.map(spectra, jnp.arange(block_count, dtype=jnp.int32))
    cross_power = jnp.transpose(cross_blocks, (1, 0, 2)).reshape(NCH, CELLS)
    diff_power = jnp.transpose(diff_blocks, (1, 0, 2)).reshape(NCH, CELLS)
    return cross_power, diff_power
```

```python
import functools
import math

import jax
import jax.numpy as jnp
from jax import lax
from jax.experimental import pallas as pl
from jax.experimental.pallas import tpu as pltpu
from jax.sharding import PartitionSpec as P

AXES = ("uv", "channel", "parity")
LANES = 128
META = 8


def send_kernel(tile_ref, chan_ref, owner_ref, place_ref, owners_ref, vis_ref, ker_ref, out_ref):
    blocks, doubled, _ = vis_ref.shape
    slots = out_ref.shape[0]

    def clear(index, carry):
        out_ref[index] = jnp.zeros(out_ref.shape[1:], out_ref.dtype)
        return carry

    lax.fori_loop(0, slots, clear, 0, unroll=8)

    place = place_ref[0]
    owner_index = place // 16
    group_local = lax.rem(place, 4)
    lane_slot = owner_index * 4 + group_local
    owners = owners_ref[...]
    tile_iota = (
        lax.broadcasted_iota(jnp.int32, owners.shape, 0) * LANES
        + lax.broadcasted_iota(jnp.int32, owners.shape, 1)
    )
    row_iota = lax.broadcasted_iota(jnp.int32, (META, LANES), 0)
    lane_iota = lax.broadcasted_iota(jnp.int32, (META, LANES), 1)
    lane_here = lane_iota // 16 == lax.rem(lane_slot, 8)
    lane_value = lax.rem(lane_iota, 16) + 1
    for block in range(blocks):
        tile = tile_ref[block]
        owner = owner_ref[tile]
        ahead = jnp.where((owners == owner) & (tile_iota < tile), 1.0, 0.0)
        rank = jnp.sum(ahead).astype(jnp.int32)
        dest = owner * (slots // 4) + rank // 2
        half = lax.rem(rank, 2)
        term = jnp.dot(
            vis_ref[block], ker_ref[block], preferred_element_type=jnp.float32
        ).astype(out_ref.dtype)
        out_ref[dest, :doubled, :] = term[:, :LANES]
        out_ref[dest, doubled : 2 * doubled, :] = term[:, LANES:]
        target = group_local * 64 + chan_ref[block] + lane_value
        meta = jnp.where(lane_here & (row_iota == half * 2 + lane_slot // 8), target, 0)
        out_ref[dest, 2 * doubled :, :] = meta.astype(jnp.float32).astype(out_ref.dtype)


def grid_kernel(got_ref, mix_ref, cross_ref, diff_ref, grid_ref, spec_ref, tail_ref):
    channels = mix_ref.shape[1]
    half = channels // 2
    spread = lax.broadcasted_iota(jnp.int32, (256, 256), 0).astype(jnp.float32) + 1.0

    def gather(chunk, carry):
        for parity in range(2):
            ids = [(u * 16 + chunk * 4 + g) * 2 + parity for u in range(4) for g in range(4)]
            meta = sum(got_ref[i, 64:, :].astype(jnp.float32) for i in ids)
            terms = jnp.concatenate(
                [
                    jnp.concatenate([got_ref[i, 16 * part : 16 * part + 16, :] for i in ids], axis=0)
                    for part in range(4)
                ],
                axis=1,
            )
            for tile in range(2):
                target = jnp.concatenate(
                    [meta[2 * tile : 2 * tile + 1], meta[2 * tile + 1 : 2 * tile + 2]], axis=1
                )
                onehot = (spread == target).astype(jnp.float32).astype(jnp.bfloat16)
                placed = jnp.dot(onehot, terms, preferred_element_type=jnp.float32).astype(
                    jnp.bfloat16
                )
                rows = pl.ds(pl.multiple_of(chunk * 256, 256), 256)
                for part in range(2):
                    grid_ref[2 * tile + part, rows, parity * 256 : parity * 256 + 256] = placed[
                        :, part * 256 : part * 256 + 256
                    ]
        return carry

    lax.fori_loop(0, channels // 256, gather, 0)

    sub = lax.broadcasted_iota(jnp.int32, (8, LANES), 0)
    flip = lax.rem(8 - sub, 8)

    for part in range(4):
        lanes = slice(part * LANES, part * LANES + LANES)
        spec_ref[...] = jnp.dot(
            mix_ref[...], grid_ref[part], preferred_element_type=jnp.float32
        )

        def powers(a_r, a_i, b_r, b_i):
            d_r = a_r - b_r
            d_i = a_i - b_i
            return a_r * b_r + a_i * b_i, d_r * d_r + d_i * d_i

        def pick(row):
            block = spec_ref[pl.ds(row, 8), :]
            return [block[:, k * LANES : (k + 1) * LANES] for k in range(4)]

        mid = pick(half)
        mid_cross, mid_diff = powers(*mid)
        tail_ref[0, half : half + 8, :] = mid_cross
        tail_ref[1, half : half + 8, :] = mid_diff

        def combine(index, carry):
            row = pl.multiple_of(index * 8, 8)
            cos = pick(row)
            sin = pick(pl.multiple_of(half + index * 8, 8))
            keep = (sub > 0) | (index > 0)
            sin = [jnp.where(keep, value, 0.0) for value in sin]
            cross, diff = powers(cos[0] + sin[1], cos[1] - sin[0], cos[2] + sin[3], cos[3] - sin[2])
            cross_ref[pl.ds(row, 8), lanes] = cross
            diff_ref[pl.ds(row, 8), lanes] = diff
            cross, diff = powers(cos[0] - sin[1], cos[1] + sin[0], cos[2] - sin[3], cos[3] + sin[2])
            tail_ref[0, pl.ds(row, 8), :] = cross
            tail_ref[1, pl.ds(row, 8), :] = diff
            return carry

        lax.fori_loop(0, half // 8, combine, 0, unroll=4)

        def reverse(index, carry):
            row = pl.multiple_of(half - index * 8, 8)
            below = pl.multiple_of(half - 8 - index * 8, 8)
            dest = pl.multiple_of(half + index * 8, 8)
            for which, out_ref in ((0, cross_ref), (1, diff_ref)):
                first = jnp.take_along_axis(tail_ref[which, pl.ds(row, 8), :], flip, axis=0)
                rest = jnp.take_along_axis(tail_ref[which, pl.ds(below, 8), :], flip, axis=0)
                out_ref[pl.ds(dest, 8), lanes] = jnp.where(sub == 0, first, rest)
            return carry

        lax.fori_loop(0, half // 8, reverse, 0, unroll=4)


def mixing(inv_cov):
    channels = inv_cov.shape[0]
    half = channels // 2
    rows = jnp.arange(half, dtype=jnp.int32)[:, None]
    cols = jnp.arange(channels, dtype=jnp.int32)[None, :]
    angles = (rows * cols % channels).astype(jnp.float32) * (2.0 * math.pi / channels)
    middle = (1 - 2 * (cols % 2)).astype(jnp.float32)
    table = jnp.concatenate(
        [jnp.cos(angles), jnp.where(rows == 0, middle, jnp.sin(angles))], axis=0
    ).astype(jnp.bfloat16)
    table = table * jnp.bfloat16(1.0 / math.sqrt(channels))
    return jnp.einsum("dc,ck->dk", table, inv_cov, preferred_element_type=jnp.float32).astype(
        jnp.bfloat16
    )


def on_device(visibility, kernel, block_tile, block_chan, tile_owner, inv_cov):
    samples = visibility[0, 0]
    weights = kernel[0, 0]
    blocks, doubled, _ = samples.shape
    devices = lax.axis_size("uv") * lax.axis_size("channel") * lax.axis_size("parity")
    channels = inv_cov.shape[0]
    cells = 512
    place = lax.axis_index(("uv", "channel")).reshape(1).astype(jnp.int32)
    smem = pl.BlockSpec(memory_space=pltpu.SMEM)
    vmem = pl.BlockSpec(memory_space=pltpu.VMEM)
    outgoing = pl.pallas_call(
        send_kernel,
        out_shape=jax.ShapeDtypeStruct((devices, 2 * doubled + META, LANES), jnp.bfloat16),
        in_specs=[smem] * 4 + [vmem] * 3,
        out_specs=vmem,
    )(
        block_tile[0, 0],
        block_chan[0, 0],
        tile_owner,
        place,
        tile_owner.reshape(-1, LANES),
        samples,
        weights,
    )
    received = lax.all_to_all(outgoing, AXES, split_axis=0, concat_axis=0, tiled=True)
    mix = mixing(inv_cov)
    shape = jax.ShapeDtypeStruct((channels, cells), jnp.float32)
    return pl.pallas_call(
        grid_kernel,
        out_shape=(shape, shape),
        in_specs=[vmem] * 2,
        out_specs=(vmem, vmem),
        scratch_shapes=[
            pltpu.VMEM((4, channels, 4 * LANES), jnp.bfloat16),
            pltpu.VMEM((channels, 4 * LANES), jnp.float32),
            pltpu.VMEM((2, channels // 2 + 8, LANES), jnp.float32),
        ],
    )(received, mix)


def solution(mesh):
    placed = (
        P("parity", "channel", "uv", None, None),
        P("parity", "channel", "uv", None, None),
        P("parity", "channel", "uv"),
        P("parity", "channel", "uv"),
        P(),
        P(),
    )
    out = P(None, AXES)
    return jax.shard_map(
        on_device, mesh=mesh, in_specs=placed, out_specs=(out, out), check_vma=False
    )
```

```python
import functools
import math

import jax
import jax.numpy as jnp
from jax import lax
from jax.experimental import pallas as pl
from jax.experimental.pallas import tpu as pltpu
from jax.sharding import PartitionSpec as P

AXES = ("uv", "channel", "parity")
LANES = 128
META = 8


def send_kernel(tile_ref, chan_ref, owner_ref, place_ref, owners_ref, vis_ref, ker_ref, out_ref):
    blocks, doubled, _ = vis_ref.shape
    slots = out_ref.shape[0]

    def clear(index, carry):
        out_ref[index] = jnp.zeros(out_ref.shape[1:], out_ref.dtype)
        return carry

    lax.fori_loop(0, slots, clear, 0, unroll=8)

    place = place_ref[0]
    owner_index = place // 16
    group_local = lax.rem(place, 4)
    lane_slot = owner_index * 4 + group_local
    owners = owners_ref[...]
    tile_iota = (
        lax.broadcasted_iota(jnp.int32, owners.shape, 0) * LANES
        + lax.broadcasted_iota(jnp.int32, owners.shape, 1)
    )
    row_iota = lax.broadcasted_iota(jnp.int32, (META, LANES), 0)
    lane_iota = lax.broadcasted_iota(jnp.int32, (META, LANES), 1)
    lane_here = lane_iota // 16 == lax.rem(lane_slot, 8)
    lane_value = lax.rem(lane_iota, 16) + 1
    for block in range(blocks):
        tile = tile_ref[block]
        owner = owner_ref[tile]
        ahead = jnp.where((owners == owner) & (tile_iota < tile), 1.0, 0.0)
        rank = jnp.sum(ahead).astype(jnp.int32)
        dest = owner * (slots // 4) + rank // 2
        half = lax.rem(rank, 2)
        term = jnp.dot(
            vis_ref[block], ker_ref[block], preferred_element_type=jnp.float32
        ).astype(out_ref.dtype)
        out_ref[dest, :doubled, :] = term[:, :LANES]
        out_ref[dest, doubled : 2 * doubled, :] = term[:, LANES:]
        target = group_local * 64 + chan_ref[block] + lane_value
        meta = jnp.where(lane_here & (row_iota == half * 2 + lane_slot // 8), target, 0)
        out_ref[dest, 2 * doubled :, :] = meta.astype(jnp.float32).astype(out_ref.dtype)


def grid_kernel(
    got_hbm, mix_hbm, cross_hbm, diff_hbm, got_ref, mix_ref, grid_ref, even_ref, odd_ref, out_ref,
    got_sem, mix_sem, out_sem,
):
    channels = mix_ref.shape[1]
    half = channels // 2

    def fetch(chunk, u):
        rows = pl.ds((u * 16 + chunk * 4) * 2, 8)
        return pltpu.make_async_copy(got_hbm.at[rows], got_ref.at[rows], got_sem.at[chunk, u])

    for chunk in range(4):
        for u in range(4):
            fetch(chunk, u).start()
    mix_copy = pltpu.make_async_copy(mix_hbm, mix_ref, mix_sem)
    mix_copy.start()

    spread = lax.broadcasted_iota(jnp.int32, (256, 256), 0).astype(jnp.float32) + 1.0

    def gather(chunk, carry):
        for u in range(4):
            fetch(chunk, u).wait()
        for parity in range(2):
            ids = [(u * 16 + chunk * 4 + g) * 2 + parity for u in range(4) for g in range(4)]
            meta = sum(got_ref[i, 64:, :].astype(jnp.float32) for i in ids)
            terms = jnp.concatenate(
                [
                    jnp.concatenate([got_ref[i, 16 * part : 16 * part + 16, :] for i in ids], axis=0)
                    for part in range(4)
                ],
                axis=1,
            )
            onehot = []
            for tile in range(2):
                target = jnp.concatenate(
                    [meta[2 * tile : 2 * tile + 1], meta[2 * tile + 1 : 2 * tile + 2]], axis=1
                )
                onehot.append((spread == target).astype(jnp.float32).astype(jnp.bfloat16))
            placed = jnp.dot(
                jnp.concatenate(onehot, axis=0), terms, preferred_element_type=jnp.float32
            ).astype(jnp.bfloat16)
            rows = pl.ds(pl.multiple_of(chunk * 256, 256), 256)
            for tile in range(2):
                for part in range(2):
                    grid_ref[2 * tile + part, rows, parity * 256 : parity * 256 + 256] = placed[
                        tile * 256 : tile * 256 + 256, part * 256 : part * 256 + 256
                    ]
        return carry

    lax.fori_loop(0, channels // 256, gather, 0)
    mix_copy.wait()

    sub = lax.broadcasted_iota(jnp.int32, (8, LANES), 0)
    flip = lax.rem(8 - sub, 8)

    def powers(a_r, a_i, b_r, b_i):
        d_r = a_r - b_r
        d_i = a_i - b_i
        return a_r * b_r + a_i * b_i, d_r * d_r + d_i * d_i

    def combine(part, spec_ref):
        for index in range(half // 8):
            row = index * 8
            cos = [spec_ref[row : row + 8, k * LANES : (k + 1) * LANES] for k in range(4)]
            sin = [
                spec_ref[half + row : half + row + 8, k * LANES : (k + 1) * LANES] for k in range(4)
            ]
            if index == 0:
                for which, power in enumerate(powers(*sin)):
                    out_ref[part, which, half : half + 1, :] = power[:1]
                sin = [jnp.where(sub > 0, value, 0.0) for value in sin]
            lower = powers(cos[0] + sin[1], cos[1] - sin[0], cos[2] + sin[3], cos[3] - sin[2])
            upper = powers(cos[0] - sin[1], cos[1] + sin[0], cos[2] - sin[3], cos[3] + sin[2])
            top = channels - row
            for which in range(2):
                out_ref[part, which, row : row + 8, :] = lower[which]
                mirrored = jnp.take_along_axis(upper[which], flip, axis=0)
                out_ref[part, which, top - 7 : top, :] = mirrored[1:]
                if index > 0:
                    out_ref[part, which, top : top + 1, :] = mirrored[:1]

    def product(part, spec_ref):
        spec_ref[...] = jnp.dot(
            mix_ref[...], grid_ref[part], preferred_element_type=jnp.float32
        )

    def send(part, which):
        target = (cross_hbm, diff_hbm)[which]
        return pltpu.make_async_copy(
            out_ref.at[part, which],
            target.at[:, pl.ds(part * LANES, LANES)],
            out_sem.at[part, which],
        )

    specs = (even_ref, odd_ref)
    product(0, specs[0])
    for part in range(4):
        if part < 3:
            product(part + 1, specs[(part + 1) % 2])
        combine(part, specs[part % 2])
        for which in range(2):
            send(part, which).start()
    for part in range(4):
        for which in range(2):
            send(part, which).wait()


def mixing(inv_cov):
    channels = inv_cov.shape[0]
    half = channels // 2
    rows = jnp.arange(half, dtype=jnp.int32)[:, None]
    cols = jnp.arange(channels, dtype=jnp.int32)[None, :]
    angles = (rows * cols % channels).astype(jnp.float32) * (2.0 * math.pi / channels)
    middle = (1 - 2 * (cols % 2)).astype(jnp.float32)
    table = jnp.concatenate(
        [jnp.cos(angles), jnp.where(rows == 0, middle, jnp.sin(angles))], axis=0
    ).astype(jnp.bfloat16)
    table = table * jnp.bfloat16(1.0 / math.sqrt(channels))
    return jnp.einsum("dc,ck->dk", table, inv_cov, preferred_element_type=jnp.float32).astype(
        jnp.bfloat16
    )


def on_device(visibility, kernel, block_tile, block_chan, tile_owner, inv_cov):
    samples = visibility[0, 0]
    weights = kernel[0, 0]
    blocks, doubled, _ = samples.shape
    devices = lax.axis_size("uv") * lax.axis_size("channel") * lax.axis_size("parity")
    channels = inv_cov.shape[0]
    cells = 512
    place = lax.axis_index(("uv", "channel")).reshape(1).astype(jnp.int32)
    smem = pl.BlockSpec(memory_space=pltpu.SMEM)
    vmem = pl.BlockSpec(memory_space=pltpu.VMEM)
    outgoing = pl.pallas_call(
        send_kernel,
        out_shape=jax.ShapeDtypeStruct((devices, 2 * doubled + META, LANES), jnp.bfloat16),
        in_specs=[smem] * 4 + [vmem] * 3,
        out_specs=vmem,
    )(
        block_tile[0, 0],
        block_chan[0, 0],
        tile_owner,
        place,
        tile_owner.reshape(-1, LANES),
        samples,
        weights,
    )
    received = lax.all_to_all(outgoing, AXES, split_axis=0, concat_axis=0, tiled=True)
    mix = mixing(inv_cov)
    shape = jax.ShapeDtypeStruct((channels, cells), jnp.float32)
    hbm = pl.BlockSpec(memory_space=pl.ANY)
    return pl.pallas_call(
        grid_kernel,
        out_shape=(shape, shape),
        in_specs=[hbm] * 2,
        out_specs=(hbm, hbm),
        scratch_shapes=[
            pltpu.VMEM(received.shape, jnp.bfloat16),
            pltpu.VMEM(mix.shape, jnp.bfloat16),
            pltpu.VMEM((4, channels, 4 * LANES), jnp.bfloat16),
            pltpu.VMEM((channels, 4 * LANES), jnp.float32),
            pltpu.VMEM((channels, 4 * LANES), jnp.float32),
            pltpu.VMEM((4, 2, channels, LANES), jnp.float32),
            pltpu.SemaphoreType.DMA((4, 4)),
            pltpu.SemaphoreType.DMA,
            pltpu.SemaphoreType.DMA((4, 2)),
        ],
    )(received, mix)


def solution(mesh):
    placed = (
        P("parity", "channel", "uv", None, None),
        P("parity", "channel", "uv", None, None),
        P("parity", "channel", "uv"),
        P("parity", "channel", "uv"),
        P(),
        P(),
    )
    out = P(None, AXES)
    return jax.shard_map(
        on_device, mesh=mesh, in_specs=placed, out_specs=(out, out), check_vma=False
    )
```

```python
import functools
import math

import jax
import jax.numpy as jnp
from jax import lax
from jax.experimental import pallas as pl
from jax.experimental.pallas import tpu as pltpu
from jax.sharding import PartitionSpec as P

AXES = ("uv", "channel", "parity")
LANES = 128
LIMIT = 48
SPARE = 8
META = 8


def send_kernel(tile_ref, chan_ref, owner_ref, place_ref, owners_ref, vis_ref, ker_ref, out_ref):
    blocks, doubled, _ = vis_ref.shape
    slots = out_ref.shape[0]

    def clear(index, carry):
        out_ref[index] = jnp.zeros(out_ref.shape[1:], out_ref.dtype)
        return carry

    lax.fori_loop(0, slots, clear, 0, unroll=8)

    place = place_ref[0]
    owner_index = place // 16
    group_local = lax.rem(place, 4)
    lane_slot = owner_index * 4 + group_local
    owners = owners_ref[...]
    tile_iota = (
        lax.broadcasted_iota(jnp.int32, owners.shape, 0) * LANES
        + lax.broadcasted_iota(jnp.int32, owners.shape, 1)
    )
    row_iota = lax.broadcasted_iota(jnp.int32, (META, LANES), 0)
    lane_iota = lax.broadcasted_iota(jnp.int32, (META, LANES), 1)
    lane_here = lane_iota // 16 == lax.rem(lane_slot, 8)
    lane_value = lax.rem(lane_iota, 16) + 1
    for block in range(blocks):
        tile = tile_ref[block]
        owner = owner_ref[tile]
        ahead = jnp.where((owners == owner) & (tile_iota < tile), 1.0, 0.0)
        rank = jnp.sum(ahead).astype(jnp.int32)
        dest = owner * (slots // 4) + rank // 2
        half = lax.rem(rank, 2)
        term = jnp.dot(
            vis_ref[block], ker_ref[block], preferred_element_type=jnp.float32
        ).astype(out_ref.dtype)
        out_ref[dest, :doubled, :] = term[:, :LANES]
        out_ref[dest, doubled : 2 * doubled, :] = term[:, LANES:]
        target = group_local * 64 + chan_ref[block] + lane_value
        meta = jnp.where(lane_here & (row_iota == half * 2 + lane_slot // 8), target, 0)
        out_ref[dest, 2 * doubled :, :] = meta.astype(jnp.float32).astype(out_ref.dtype)


def grid_kernel(
    got_ref, mix_hbm, cross_hbm, diff_hbm, mix_ref, grid_ref, even_ref, odd_ref, out_ref,
    mix_sem, out_sem,
):
    channels = mix_ref.shape[1]
    half = channels // 2

    mix_copy = pltpu.make_async_copy(mix_hbm.at[0], mix_ref, mix_sem)
    mix_copy.start()

    spread = lax.broadcasted_iota(jnp.int32, (256, 256), 0).astype(jnp.float32) + 1.0

    def gather(chunk, carry):
        for parity in range(2):
            ids = [(u * 16 + chunk * 4 + g) * 2 + parity for u in range(4) for g in range(4)]
            meta = sum(got_ref[i, 64:, :].astype(jnp.float32) for i in ids)
            terms = jnp.concatenate(
                [
                    jnp.concatenate([got_ref[i, 16 * part : 16 * part + 16, :] for i in ids], axis=0)
                    for part in range(4)
                ],
                axis=1,
            )
            onehot = []
            for tile in range(2):
                target = jnp.concatenate(
                    [meta[2 * tile : 2 * tile + 1], meta[2 * tile + 1 : 2 * tile + 2]], axis=1
                )
                onehot.append((spread == target).astype(jnp.float32).astype(jnp.bfloat16))
            placed = jnp.dot(
                jnp.concatenate(onehot, axis=0), terms, preferred_element_type=jnp.float32
            ).astype(jnp.bfloat16)
            rows = pl.ds(pl.multiple_of(chunk * 256, 256), 256)
            for tile in range(2):
                for part in range(2):
                    grid_ref[2 * tile + part, rows, parity * 256 : parity * 256 + 256] = placed[
                        tile * 256 : tile * 256 + 256, part * 256 : part * 256 + 256
                    ]
        return carry

    lax.fori_loop(0, channels // 256, gather, 0)
    mix_copy.wait()

    sub = lax.broadcasted_iota(jnp.int32, (8, LANES), 0)
    flip = lax.rem(8 - sub, 8)

    def powers(a_r, a_i, b_r, b_i):
        d_r = a_r - b_r
        d_i = a_i - b_i
        return a_r * b_r + a_i * b_i, d_r * d_r + d_i * d_i

    def combine(part, spec_ref):
        for index in range(half // 8):
            row = index * 8
            cos = [spec_ref[row : row + 8, k * LANES : (k + 1) * LANES] for k in range(4)]
            sin = [
                spec_ref[half + row : half + row + 8, k * LANES : (k + 1) * LANES] for k in range(4)
            ]
            if index == 0:
                for which, power in enumerate(powers(*sin)):
                    out_ref[part, which, half : half + 1, :] = power[:1]
                sin = [jnp.where(sub > 0, value, 0.0) for value in sin]
            lower = powers(cos[0] + sin[1], cos[1] - sin[0], cos[2] + sin[3], cos[3] - sin[2])
            upper = powers(cos[0] - sin[1], cos[1] + sin[0], cos[2] - sin[3], cos[3] + sin[2])
            top = channels - row
            for which in range(2):
                out_ref[part, which, row : row + 8, :] = lower[which]
                mirrored = jnp.take_along_axis(upper[which], flip, axis=0)
                out_ref[part, which, top - 7 : top, :] = mirrored[1:]
                if index > 0:
                    out_ref[part, which, top : top + 1, :] = mirrored[:1]

    def product(part, spec_ref):
        spec_ref[...] = jnp.dot(
            mix_ref[...], grid_ref[part], preferred_element_type=jnp.float32
        )

    def send(part, which):
        target = (cross_hbm, diff_hbm)[which]
        return pltpu.make_async_copy(
            out_ref.at[part, which],
            target.at[:, pl.ds(part * LANES, LANES)],
            out_sem.at[part, which],
        )

    specs = (even_ref, odd_ref)
    product(0, specs[0])
    for part in range(4):
        if part < 3:
            product(part + 1, specs[(part + 1) % 2])
        combine(part, specs[part % 2])
        for which in range(2):
            send(part, which).start()
    for part in range(4):
        for which in range(2):
            send(part, which).wait()


def mix_kernel(cov_ref, out_hbm, table_ref, out_ref, sem):
    channels = cov_ref.shape[0]
    half = channels // 2
    inner = 32
    scale = 1.0 / math.sqrt(channels)

    def angles(count, step):
        rows = lax.broadcasted_iota(jnp.int32, (count, channels), 0) * step
        cols = lax.broadcasted_iota(jnp.int32, (count, channels), 1)
        return lax.rem(rows * cols, channels).astype(jnp.float32) * (2.0 * math.pi / channels)

    outer_angles = angles(half // inner, inner)
    inner_angles = angles(inner, 1)
    outer_cos, outer_sin = jnp.cos(outer_angles) * scale, jnp.sin(outer_angles) * scale
    inner_cos, inner_sin = jnp.cos(inner_angles), jnp.sin(inner_angles)
    for index in range(half // inner):
        cos, sin = outer_cos[index : index + 1], outer_sin[index : index + 1]
        lower = cos * inner_cos - sin * inner_sin
        upper = sin * inner_cos + cos * inner_sin
        if index == 0:
            rows = lax.broadcasted_iota(jnp.int32, upper.shape, 0)
            odd = lax.rem(lax.broadcasted_iota(jnp.int32, upper.shape, 1), 2)
            middle = (1 - 2 * odd).astype(jnp.float32) * scale
            upper = jnp.where(rows == 0, middle, upper)
        table_ref[index * inner : index * inner + inner, :] = lower.astype(table_ref.dtype)
        table_ref[half + index * inner : half + index * inner + inner, :] = upper.astype(
            table_ref.dtype
        )
    out_ref[...] = jnp.dot(
        table_ref[...], cov_ref[...], preferred_element_type=jnp.float32
    ).astype(out_ref.dtype)
    copy = pltpu.make_async_copy(out_ref, out_hbm.at[0], sem)
    copy.start()
    copy.wait()


def on_device(visibility, kernel, block_tile, block_chan, tile_owner, inv_cov):
    samples = visibility[0, 0]
    weights = kernel[0, 0]
    blocks, doubled, _ = samples.shape
    devices = lax.axis_size("uv") * lax.axis_size("channel") * lax.axis_size("parity")
    channels = inv_cov.shape[0]
    cells = 512
    place = lax.axis_index(("uv", "channel")).reshape(1).astype(jnp.int32)
    smem = pl.BlockSpec(memory_space=pltpu.SMEM)
    vmem = pl.BlockSpec(memory_space=pltpu.VMEM)
    hbm = pl.BlockSpec(memory_space=pl.ANY)
    outgoing = pl.pallas_call(
        send_kernel,
        out_shape=jax.ShapeDtypeStruct((devices, 2 * doubled + META, LANES), jnp.bfloat16),
        in_specs=[smem] * 4 + [vmem] * 3,
        out_specs=vmem,
    )(
        block_tile[0, 0],
        block_chan[0, 0],
        tile_owner,
        place,
        tile_owner.reshape(-1, LANES),
        samples,
        weights,
    )
    received = lax.all_to_all(outgoing, AXES, split_axis=0, concat_axis=0, tiled=True)
    mix = pl.pallas_call(
        mix_kernel,
        out_shape=jax.ShapeDtypeStruct((SPARE,) + inv_cov.shape, inv_cov.dtype),
        in_specs=[vmem],
        out_specs=hbm,
        scratch_shapes=[
            pltpu.VMEM(inv_cov.shape, inv_cov.dtype),
            pltpu.VMEM(inv_cov.shape, inv_cov.dtype),
            pltpu.SemaphoreType.DMA,
        ],
        cost_estimate=pl.CostEstimate(
            flops=2 * channels**3, bytes_accessed=4 * channels**2, transcendentals=0
        ),
    )(inv_cov)
    shape = jax.ShapeDtypeStruct((channels, cells), jnp.float32)
    return pl.pallas_call(
        grid_kernel,
        out_shape=(shape, shape),
        in_specs=[vmem, hbm],
        out_specs=(hbm, hbm),
        scratch_shapes=[
            pltpu.VMEM(inv_cov.shape, jnp.bfloat16),
            pltpu.VMEM((4, channels, 4 * LANES), jnp.bfloat16),
            pltpu.VMEM((channels, 4 * LANES), jnp.float32),
            pltpu.VMEM((channels, 4 * LANES), jnp.float32),
            pltpu.VMEM((4, 2, channels, LANES), jnp.float32),
            pltpu.SemaphoreType.DMA,
            pltpu.SemaphoreType.DMA((4, 2)),
        ],
        compiler_params=pltpu.CompilerParams(vmem_limit_bytes=LIMIT * 2**20),
    )(received, mix)


def solution(mesh):
    placed = (
        P("parity", "channel", "uv", None, None),
        P("parity", "channel", "uv", None, None),
        P("parity", "channel", "uv"),
        P("parity", "channel", "uv"),
        P(),
        P(),
    )
    out = P(None, AXES)
    return jax.shard_map(
        on_device, mesh=mesh, in_specs=placed, out_specs=(out, out), check_vma=False
    )
```

```python
import functools
import math

import jax
import jax.numpy as jnp
from jax import lax
from jax.experimental import pallas as pl
from jax.experimental.pallas import tpu as pltpu
from jax.sharding import PartitionSpec as P

AXES = ("uv", "channel", "parity")
LANES = 128
LIMIT = 48
SPARE = 8
PAIR = 2


def rows_of(ref, slot):
    return ref.at[slot].reshape(ref.shape[1] * PAIR, LANES)


def send_kernel(
    tile_ref, chan_ref, owner_ref, place_ref, owners_ref, vis_hbm, ker_hbm, out_ref,
    vis_ref, ker_ref, zero_ref, vis_sem, ker_sem, zero_sem,
):
    blocks, doubled, _ = vis_ref.shape
    slots = out_ref.shape[0]
    clear = zero_ref.shape[0]
    loads = ker_sem.shape[0]
    size = blocks // loads

    vis_copy = pltpu.make_async_copy(vis_hbm, vis_ref, vis_sem)
    vis_copy.start()
    ker_copies = []
    for load in range(loads):
        span = pl.ds(load * size, size)
        ker_copies.append(
            pltpu.make_async_copy(ker_hbm.at[span], ker_ref.at[span], ker_sem.at[load])
        )
        ker_copies[-1].start()

    zero_ref[...] = jnp.zeros(zero_ref.shape, zero_ref.dtype)
    zero_copies = []
    for index in range(slots // clear):
        target = out_ref.at[pl.ds(index * clear, clear)]
        zero_copies.append(pltpu.make_async_copy(zero_ref, target, zero_sem.at[index]))
        zero_copies[-1].start()

    place = place_ref[0]
    group_local = lax.rem(place, 4)
    lane_slot = place // 16 * 4 + group_local
    owners = owners_ref[...]
    tile_iota = (
        lax.broadcasted_iota(jnp.int32, owners.shape, 0) * LANES
        + lax.broadcasted_iota(jnp.int32, owners.shape, 1)
    )
    row_iota = lax.broadcasted_iota(jnp.int32, (PAIR, LANES), 0)
    lane_iota = lax.broadcasted_iota(jnp.int32, (PAIR, LANES), 1)
    lane_here = (lane_iota // 16 == lax.rem(lane_slot, 8)) & (row_iota == lane_slot // 8)
    lane_value = lax.rem(lane_iota, 16) + 1 + group_local * 64
    dests, metas = [], []
    for block in range(blocks):
        tile = tile_ref[block]
        owner = owner_ref[tile]
        ahead = jnp.where((owners == owner) & (tile_iota < tile), 1.0, 0.0)
        rank = jnp.sum(ahead).astype(jnp.int32)
        dests.append(owner * (slots // 4) + rank // 2)
        target = (chan_ref[block] + lane_value) * (1 - 2 * lax.rem(rank, 2))
        metas.append(jnp.where(lane_here, target, 0).astype(jnp.float32).astype(out_ref.dtype))

    vis_copy.wait()
    for copy in zero_copies:
        copy.wait()
    for load in range(loads):
        ker_copies[load].wait()
        for block in range(load * size, load * size + size):
            term = jnp.dot(
                vis_ref[block], ker_ref[block], preferred_element_type=jnp.float32
            ).astype(out_ref.dtype)
            slot = rows_of(out_ref, dests[block])
            slot[:doubled, :] = term[:, :LANES]
            slot[doubled : 2 * doubled, :] = term[:, LANES:]
            slot[2 * doubled :, :] = metas[block]


def grid_kernel(
    got_ref, mix_hbm, cross_hbm, diff_hbm, mix_ref, grid_ref, out_ref,
    mix_sem, out_sem,
):
    channels = mix_ref.shape[1]
    half = channels // 2

    mix_copy = pltpu.make_async_copy(mix_hbm.at[0], mix_ref, mix_sem)
    mix_copy.start()

    spread = lax.broadcasted_iota(jnp.int32, (256, 256), 0).astype(jnp.float32) + 1.0

    height = 66
    step = 8 * height

    def gather(chunk, carry):
        near = got_ref.at[pl.ds(pl.multiple_of(chunk * step, 16), got_ref.shape[0] - 3 * step)]
        for parity in range(2):
            ids = [(u * 16 + g) * 2 + parity for u in range(4) for g in range(4)]
            meta = sum(near[i * height + 64 : i * height + 66, :].astype(jnp.float32) for i in ids)
            terms = jnp.concatenate(
                [
                    jnp.concatenate(
                        [
                            near[i * height + 16 * part : i * height + 16 * part + 16, :]
                            for i in ids
                        ],
                        axis=0,
                    )
                    for part in range(4)
                ],
                axis=1,
            )
            target = jnp.concatenate([meta[:1], meta[1:]], axis=1)
            onehot = [
                (spread == signed).astype(jnp.float32).astype(jnp.bfloat16)
                for signed in (target, -target)
            ]
            placed = jnp.dot(
                jnp.concatenate(onehot, axis=0), terms, preferred_element_type=jnp.float32
            ).astype(jnp.bfloat16)
            rows = pl.ds(pl.multiple_of(chunk * 256, 256), 256)
            for tile in range(2):
                for part in range(2):
                    grid_ref[2 * tile + part, rows, parity * 256 : parity * 256 + 256] = placed[
                        tile * 256 : tile * 256 + 256, part * 256 : part * 256 + 256
                    ]
        return carry

    lax.fori_loop(0, channels // 256, gather, 0)
    mix_copy.wait()

    sub = lax.broadcasted_iota(jnp.int32, (8, LANES), 0)
    flip = lax.rem(8 - sub, 8)

    def powers(a_r, a_i, b_r, b_i):
        d_r = a_r - b_r
        d_i = a_i - b_i
        return a_r * b_r + a_i * b_i, d_r * d_r + d_i * d_i

    def combine(part, spec):
        for index in range(half // 8):
            row = index * 8
            cos = [spec[row : row + 8, k * LANES : (k + 1) * LANES] for k in range(4)]
            sin = [spec[half + row : half + row + 8, k * LANES : (k + 1) * LANES] for k in range(4)]
            if index == 0:
                for which, power in enumerate(powers(*sin)):
                    out_ref[part, which, half : half + 1, :] = power[:1]
                sin = [jnp.where(sub > 0, value, 0.0) for value in sin]
            lower = powers(cos[0] + sin[1], cos[1] - sin[0], cos[2] + sin[3], cos[3] - sin[2])
            upper = powers(cos[0] - sin[1], cos[1] + sin[0], cos[2] - sin[3], cos[3] + sin[2])
            top = channels - row
            for which in range(2):
                out_ref[part, which, row : row + 8, :] = lower[which]
                mirrored = jnp.take_along_axis(upper[which], flip, axis=0, mode="promise_in_bounds")
                out_ref[part, which, top - 7 : top, :] = mirrored[1:]
                if index > 0:
                    out_ref[part, which, top : top + 1, :] = mirrored[:1]

    def product(part):
        return jnp.dot(mix_ref[...], grid_ref[part], preferred_element_type=jnp.float32)

    def send(part, which):
        target = (cross_hbm, diff_hbm)[which]
        return pltpu.make_async_copy(
            out_ref.at[part, which],
            target.at[:, pl.ds(part * LANES, LANES)],
            out_sem.at[part, which],
        )

    for part in range(4):
        combine(part, product(part))
        if part == 2:
            for done in range(3):
                for which in range(2):
                    send(done, which).start()
    for which in range(2):
        send(3, which).start()
    for part in range(4):
        for which in range(2):
            send(part, which).wait()


def mix_kernel(cov_ref, out_hbm, table_ref, out_ref, sem):
    channels = cov_ref.shape[0]
    half = channels // 2
    inner = 32
    scale = 1.0 / math.sqrt(channels)

    def angles(count, step):
        rows = lax.broadcasted_iota(jnp.int32, (count, channels), 0) * step
        cols = lax.broadcasted_iota(jnp.int32, (count, channels), 1)
        return lax.rem(rows * cols, channels).astype(jnp.float32) * (2.0 * math.pi / channels)

    outer_angles = angles(half // inner, inner)
    inner_angles = angles(inner, 1)
    outer_cos, outer_sin = jnp.cos(outer_angles) * scale, jnp.sin(outer_angles) * scale
    inner_cos, inner_sin = jnp.cos(inner_angles), jnp.sin(inner_angles)
    for index in range(half // inner):
        cos, sin = outer_cos[index : index + 1], outer_sin[index : index + 1]
        lower = cos * inner_cos - sin * inner_sin
        upper = sin * inner_cos + cos * inner_sin
        if index == 0:
            rows = lax.broadcasted_iota(jnp.int32, upper.shape, 0)
            odd = lax.rem(lax.broadcasted_iota(jnp.int32, upper.shape, 1), 2)
            middle = (1 - 2 * odd).astype(jnp.float32) * scale
            upper = jnp.where(rows == 0, middle, upper)
        table_ref[index * inner : index * inner + inner, :] = lower.astype(table_ref.dtype)
        table_ref[half + index * inner : half + index * inner + inner, :] = upper.astype(
            table_ref.dtype
        )
    out_ref[...] = jnp.dot(
        table_ref[...], cov_ref[...], preferred_element_type=jnp.float32
    ).astype(out_ref.dtype)
    copy = pltpu.make_async_copy(out_ref, out_hbm.at[0], sem)
    copy.start()
    copy.wait()


def on_device(visibility, kernel, block_tile, block_chan, tile_owner, inv_cov):
    samples = visibility[0, 0]
    weights = kernel[0, 0]
    blocks, doubled, _ = samples.shape
    devices = lax.axis_size("uv") * lax.axis_size("channel") * lax.axis_size("parity")
    channels = inv_cov.shape[0]
    cells = 512
    place = lax.axis_index(("uv", "channel")).reshape(1).astype(jnp.int32)
    smem = pl.BlockSpec(memory_space=pltpu.SMEM)
    vmem = pl.BlockSpec(memory_space=pltpu.VMEM)
    hbm = pl.BlockSpec(memory_space=pl.ANY)
    outgoing = pl.pallas_call(
        send_kernel,
        out_shape=jax.ShapeDtypeStruct((devices, doubled + 1, PAIR, LANES), jnp.bfloat16),
        in_specs=[smem] * 4 + [vmem] + [hbm] * 2,
        out_specs=vmem,
        scratch_shapes=[
            pltpu.VMEM(samples.shape, samples.dtype),
            pltpu.VMEM(weights.shape, weights.dtype),
            pltpu.VMEM((16, doubled + 1, PAIR, LANES), jnp.bfloat16),
            pltpu.SemaphoreType.DMA,
            pltpu.SemaphoreType.DMA((2,)),
            pltpu.SemaphoreType.DMA((devices // 16,)),
        ],
    )(
        block_tile[0, 0],
        block_chan[0, 0],
        tile_owner,
        place,
        tile_owner.reshape(-1, LANES),
        samples,
        weights,
    )
    received = lax.all_to_all(outgoing, AXES, split_axis=0, concat_axis=0, tiled=True)
    mix = pl.pallas_call(
        mix_kernel,
        out_shape=jax.ShapeDtypeStruct((SPARE,) + inv_cov.shape, inv_cov.dtype),
        in_specs=[vmem],
        out_specs=hbm,
        scratch_shapes=[
            pltpu.VMEM(inv_cov.shape, inv_cov.dtype),
            pltpu.VMEM(inv_cov.shape, inv_cov.dtype),
            pltpu.SemaphoreType.DMA,
        ],
        cost_estimate=pl.CostEstimate(
            flops=2 * channels**3, bytes_accessed=4 * channels**2, transcendentals=0
        ),
    )(inv_cov)
    shape = jax.ShapeDtypeStruct((channels, cells), jnp.float32)
    return pl.pallas_call(
        grid_kernel,
        out_shape=(shape, shape),
        in_specs=[vmem, hbm],
        out_specs=(hbm, hbm),
        scratch_shapes=[
            pltpu.VMEM(inv_cov.shape, jnp.bfloat16),
            pltpu.VMEM((4, channels, 4 * LANES), jnp.bfloat16),
            pltpu.VMEM((4, 2, channels, LANES), jnp.float32),
            pltpu.SemaphoreType.DMA,
            pltpu.SemaphoreType.DMA((4, 2)),
        ],
        compiler_params=pltpu.CompilerParams(vmem_limit_bytes=LIMIT * 2**20),
    )(received.reshape(-1, LANES), mix)


def solution(mesh):
    placed = (
        P("parity", "channel", "uv", None, None),
        P("parity", "channel", "uv", None, None),
        P("parity", "channel", "uv"),
        P("parity", "channel", "uv"),
        P(),
        P(),
    )
    out = P(None, AXES)
    return jax.shard_map(
        on_device, mesh=mesh, in_specs=placed, out_specs=(out, out), check_vma=False
    )
```

```python
import functools
import math

import jax
import jax.numpy as jnp
from jax import lax
from jax.experimental import pallas as pl
from jax.experimental.pallas import tpu as pltpu
from jax.sharding import PartitionSpec as P

AXES = ("uv", "channel", "parity")
LANES = 128
LIMIT = 48
SPARE = 8
PAIR = 2


def rows_of(ref, slot):
    return ref.at[slot].reshape(ref.shape[1] * PAIR, LANES)


def send_kernel(
    tile_ref, chan_ref, owner_ref, place_ref, owners_ref, vis_hbm, ker_hbm, out_ref,
    vis_ref, ker_ref, zero_ref, vis_sem, ker_sem, zero_sem,
):
    blocks, doubled, _ = vis_ref.shape
    slots = out_ref.shape[0]
    clear = zero_ref.shape[0]
    loads = ker_sem.shape[0]
    size = blocks // loads

    vis_copy = pltpu.make_async_copy(vis_hbm, vis_ref, vis_sem)
    vis_copy.start()
    ker_copies = []
    for load in range(loads):
        span = pl.ds(load * size, size)
        ker_copies.append(
            pltpu.make_async_copy(ker_hbm.at[span], ker_ref.at[span], ker_sem.at[load])
        )
        ker_copies[-1].start()

    zero_ref[...] = jnp.zeros(zero_ref.shape, zero_ref.dtype)
    zero_copies = []
    for index in range(slots // clear):
        target = out_ref.at[pl.ds(index * clear, clear)]
        zero_copies.append(pltpu.make_async_copy(zero_ref, target, zero_sem.at[index]))
        zero_copies[-1].start()

    place = place_ref[0]
    group_local = lax.rem(place, 4)
    lane_slot = place // 16 * 4 + group_local
    owners = owners_ref[...]
    tile_iota = (
        lax.broadcasted_iota(jnp.int32, owners.shape, 0) * LANES
        + lax.broadcasted_iota(jnp.int32, owners.shape, 1)
    )
    row_iota = lax.broadcasted_iota(jnp.int32, (PAIR, LANES), 0)
    lane_iota = lax.broadcasted_iota(jnp.int32, (PAIR, LANES), 1)
    lane_here = (lane_iota // 16 == lax.rem(lane_slot, 8)) & (row_iota == lane_slot // 8)
    lane_value = lax.rem(lane_iota, 16) + 1 + group_local * 64
    dests, metas = [], []
    for block in range(blocks):
        tile = tile_ref[block]
        owner = owner_ref[tile]
        ahead = jnp.where((owners == owner) & (tile_iota < tile), 1.0, 0.0)
        rank = jnp.sum(ahead).astype(jnp.int32)
        dests.append(owner * (slots // 4) + rank // 2)
        target = (chan_ref[block] + lane_value) * (1 - 2 * lax.rem(rank, 2))
        metas.append(jnp.where(lane_here, target, 0).astype(jnp.float32).astype(out_ref.dtype))

    vis_copy.wait()
    for copy in zero_copies:
        copy.wait()
    for load in range(loads):
        ker_copies[load].wait()
        for block in range(load * size, load * size + size):
            term = jnp.dot(
                vis_ref[block], ker_ref[block], preferred_element_type=jnp.float32
            ).astype(out_ref.dtype)
            slot = rows_of(out_ref, dests[block])
            slot[:doubled, :] = term[:, :LANES]
            slot[doubled : 2 * doubled, :] = term[:, LANES:]
            slot[2 * doubled :, :] = metas[block]


def grid_kernel(
    got_ref, mix_hbm, cross_hbm, diff_hbm, mix_ref, grid_ref, out_ref,
    mix_sem, out_sem,
):
    channels = mix_ref.shape[1]
    half = channels // 2

    mix_copy = pltpu.make_async_copy(mix_hbm.at[0], mix_ref, mix_sem)
    mix_copy.start()

    spread = lax.broadcasted_iota(jnp.int32, (256, 256), 0).astype(jnp.float32) + 1.0

    height = 66
    step = 8 * height

    def gather(chunk, carry):
        near = got_ref.at[pl.ds(pl.multiple_of(chunk * step, 16), got_ref.shape[0] - 3 * step)]
        for parity in range(2):
            ids = [(u * 16 + g) * 2 + parity for u in range(4) for g in range(4)]
            meta = sum(near[i * height + 64 : i * height + 66, :].astype(jnp.float32) for i in ids)
            terms = jnp.concatenate(
                [
                    jnp.concatenate(
                        [
                            near[i * height + 16 * part : i * height + 16 * part + 16, :]
                            for i in ids
                        ],
                        axis=0,
                    )
                    for part in range(4)
                ],
                axis=1,
            )
            target = jnp.concatenate([meta[:1], meta[1:]], axis=1)
            onehot = [
                (spread == signed).astype(jnp.float32).astype(jnp.bfloat16)
                for signed in (target, -target)
            ]
            placed = jnp.dot(
                jnp.concatenate(onehot, axis=0), terms, preferred_element_type=jnp.float32
            ).astype(jnp.bfloat16)
            rows = pl.ds(pl.multiple_of(chunk * 256, 256), 256)
            for tile in range(2):
                for part in range(2):
                    grid_ref[2 * tile + part, rows, parity * 256 : parity * 256 + 256] = placed[
                        tile * 256 : tile * 256 + 256, part * 256 : part * 256 + 256
                    ]
        return carry

    lax.fori_loop(0, channels // 256, gather, 0)
    mix_copy.wait()

    sub = lax.broadcasted_iota(jnp.int32, (8, LANES), 0)
    flip = lax.rem(8 - sub, 8)

    def powers(a_r, a_i, b_r, b_i):
        d_r = a_r - b_r
        d_i = a_i - b_i
        return a_r * b_r + a_i * b_i, d_r * d_r + d_i * d_i

    size = half // 2

    def combine(part, block, spec):
        for index in range(size // 8):
            local = index * 8
            row = block * size + local
            cos = [spec[local : local + 8, k * LANES : (k + 1) * LANES] for k in range(4)]
            sin = [
                spec[size + local : size + local + 8, k * LANES : (k + 1) * LANES] for k in range(4)
            ]
            if row == 0:
                for which, power in enumerate(powers(*sin)):
                    out_ref[part, which, half : half + 1, :] = power[:1]
                sin = [jnp.where(sub > 0, value, 0.0) for value in sin]
            lower = powers(cos[0] + sin[1], cos[1] - sin[0], cos[2] + sin[3], cos[3] - sin[2])
            upper = powers(cos[0] - sin[1], cos[1] + sin[0], cos[2] - sin[3], cos[3] + sin[2])
            top = channels - row
            for which in range(2):
                out_ref[part, which, row : row + 8, :] = lower[which]
                mirrored = jnp.take_along_axis(upper[which], flip, axis=0, mode="promise_in_bounds")
                out_ref[part, which, top - 7 : top, :] = mirrored[1:]
                if row > 0:
                    out_ref[part, which, top : top + 1, :] = mirrored[:1]

    def product(part, block):
        first = block * size
        rows = jnp.concatenate(
            [mix_ref[first : first + size, :], mix_ref[half + first : half + first + size, :]],
            axis=0,
        )
        return jnp.dot(rows, grid_ref[part], preferred_element_type=jnp.float32)

    def send(part, which):
        target = (cross_hbm, diff_hbm)[which]
        return pltpu.make_async_copy(
            out_ref.at[part, which],
            target.at[:, pl.ds(part * LANES, LANES)],
            out_sem.at[part, which],
        )

    work = [(part, block) for part in range(4) for block in range(2)]
    ahead = product(*work[0])
    for index, (part, block) in enumerate(work):
        spec = ahead
        if index + 1 < len(work):
            ahead = product(*work[index + 1])
        combine(part, block, spec)
        if index == 5:
            for done in range(3):
                for which in range(2):
                    send(done, which).start()
    for which in range(2):
        send(3, which).start()
    for part in range(4):
        for which in range(2):
            send(part, which).wait()


def mix_kernel(cov_ref, out_hbm, table_ref, out_ref, sem):
    channels = cov_ref.shape[0]
    half = channels // 2
    inner = 32
    scale = 1.0 / math.sqrt(channels)

    def angles(count, step):
        rows = lax.broadcasted_iota(jnp.int32, (count, channels), 0) * step
        cols = lax.broadcasted_iota(jnp.int32, (count, channels), 1)
        return lax.rem(rows * cols, channels).astype(jnp.float32) * (2.0 * math.pi / channels)

    outer_angles = angles(half // inner, inner)
    inner_angles = angles(inner, 1)
    outer_cos, outer_sin = jnp.cos(outer_angles) * scale, jnp.sin(outer_angles) * scale
    inner_cos, inner_sin = jnp.cos(inner_angles), jnp.sin(inner_angles)
    for index in range(half // inner):
        cos, sin = outer_cos[index : index + 1], outer_sin[index : index + 1]
        lower = cos * inner_cos - sin * inner_sin
        upper = sin * inner_cos + cos * inner_sin
        if index == 0:
            rows = lax.broadcasted_iota(jnp.int32, upper.shape, 0)
            odd = lax.rem(lax.broadcasted_iota(jnp.int32, upper.shape, 1), 2)
            middle = (1 - 2 * odd).astype(jnp.float32) * scale
            upper = jnp.where(rows == 0, middle, upper)
        table_ref[index * inner : index * inner + inner, :] = lower.astype(table_ref.dtype)
        table_ref[half + index * inner : half + index * inner + inner, :] = upper.astype(
            table_ref.dtype
        )
    out_ref[...] = jnp.dot(
        table_ref[...], cov_ref[...], preferred_element_type=jnp.float32
    ).astype(out_ref.dtype)
    copy = pltpu.make_async_copy(out_ref, out_hbm.at[0], sem)
    copy.start()
    copy.wait()


def on_device(visibility, kernel, block_tile, block_chan, tile_owner, inv_cov):
    samples = visibility[0, 0]
    weights = kernel[0, 0]
    blocks, doubled, _ = samples.shape
    devices = lax.axis_size("uv") * lax.axis_size("channel") * lax.axis_size("parity")
    channels = inv_cov.shape[0]
    cells = 512
    place = lax.axis_index(("uv", "channel")).reshape(1).astype(jnp.int32)
    smem = pl.BlockSpec(memory_space=pltpu.SMEM)
    vmem = pl.BlockSpec(memory_space=pltpu.VMEM)
    hbm = pl.BlockSpec(memory_space=pl.ANY)
    outgoing = pl.pallas_call(
        send_kernel,
        out_shape=jax.ShapeDtypeStruct((devices, doubled + 1, PAIR, LANES), jnp.bfloat16),
        in_specs=[smem] * 4 + [vmem] + [hbm] * 2,
        out_specs=vmem,
        scratch_shapes=[
            pltpu.VMEM(samples.shape, samples.dtype),
            pltpu.VMEM(weights.shape, weights.dtype),
            pltpu.VMEM((16, doubled + 1, PAIR, LANES), jnp.bfloat16),
            pltpu.SemaphoreType.DMA,
            pltpu.SemaphoreType.DMA((2,)),
            pltpu.SemaphoreType.DMA((devices // 16,)),
        ],
    )(
        block_tile[0, 0],
        block_chan[0, 0],
        tile_owner,
        place,
        tile_owner.reshape(-1, LANES),
        samples,
        weights,
    )
    received = lax.all_to_all(outgoing, AXES, split_axis=0, concat_axis=0, tiled=True)
    mix = pl.pallas_call(
        mix_kernel,
        out_shape=jax.ShapeDtypeStruct((SPARE,) + inv_cov.shape, inv_cov.dtype),
        in_specs=[vmem],
        out_specs=hbm,
        scratch_shapes=[
            pltpu.VMEM(inv_cov.shape, inv_cov.dtype),
            pltpu.VMEM(inv_cov.shape, inv_cov.dtype),
            pltpu.SemaphoreType.DMA,
        ],
        cost_estimate=pl.CostEstimate(
            flops=2 * channels**3, bytes_accessed=4 * channels**2, transcendentals=0
        ),
    )(inv_cov)
    shape = jax.ShapeDtypeStruct((channels, cells), jnp.float32)
    return pl.pallas_call(
        grid_kernel,
        out_shape=(shape, shape),
        in_specs=[vmem, hbm],
        out_specs=(hbm, hbm),
        scratch_shapes=[
            pltpu.VMEM(inv_cov.shape, jnp.bfloat16),
            pltpu.VMEM((4, channels, 4 * LANES), jnp.bfloat16),
            pltpu.VMEM((4, 2, channels, LANES), jnp.float32),
            pltpu.SemaphoreType.DMA,
            pltpu.SemaphoreType.DMA((4, 2)),
        ],
        compiler_params=pltpu.CompilerParams(vmem_limit_bytes=LIMIT * 2**20),
    )(received.reshape(-1, LANES), mix)


def solution(mesh):
    placed = (
        P("parity", "channel", "uv", None, None),
        P("parity", "channel", "uv", None, None),
        P("parity", "channel", "uv"),
        P("parity", "channel", "uv"),
        P(),
        P(),
    )
    out = P(None, AXES)
    return jax.shard_map(
        on_device, mesh=mesh, in_specs=placed, out_specs=(out, out), check_vma=False
    )
```
